32 devices in a mesh: clips: 2 (over y), tm: 4 (over z), rows: 4 (over x, core).
Axes of the slice: x: 2, y: 2, z: 4, core: 2. Of those that a mesh axis runs over, the one named last changes fastest.
Arguments:
- latents: bfloat16 [32, 8, 192, 128], P(('clips', 'tm'), 'rows'), parts along dimension 0, may hold values from -6 to 6
- conv_weight: bfloat16 [3, 27, 192, 192], replicated, may hold values from -0.078125 to 0.078125
- norm_gains: float32 [3, 192], replicated, may hold values from 0.5 to 1.5
- biases: float32 [3, 192], replicated, may hold values from -3 to 3
Outputs:
- decoded: bfloat16 [32, 8, 192, 128], P(('clips', 'tm'), 'rows'), parts along dimension 0
The draws below stay inside these ranges and needn't reach their ends.
There are 2 independent parts, one for each index of `clips`. The reference program is written for one: setup_inputs(seed, part) draws one part's arguments, and reference() takes and returns one part's arrays. A program takes and returns all parts, laid end to end along the dimension named above; an argument that names none is the same for every part. Nothing has to cross between parts.
All inputs are finite; a program needn't handle non-finite values.
Results may differ from the reference program's by a relative error of at most 0.011.
Values may be sent and summed in bfloat16 or wider, within the bound.
A program may use at most 64 MiB of HBM per device.

```python
import jax
import jax.numpy as jnp
from jax import lax

C = 192
W = 128
LAYERS = 3
FRAMES = 16
HEIGHT = 8


def block_levels(stream_key, dims, pieces, low, top_value):
    def one(axis_at, parts):
        draws = jax.random.uniform(jax.random.fold_in(jax.random.fold_in(stream_key, 6), axis_at), (parts,), jnp.float32, low / len(pieces), top_value / len(pieces))
        return jnp.repeat(jnp.exp(draws), dims[axis_at] // parts).reshape((-1,) + (1,) * (len(dims) - axis_at - 1))

    gain = one(*pieces[0])
    for cut in pieces[1:]:
        gain = gain * one(*cut)
    return gain


def normal_values(stream_key, shape, spread, bound, split=(), held_as=jnp.bfloat16):
    entries = jax.random.normal(stream_key, shape, jnp.float32) * spread
    if len(split) > 0:
        entries = block_levels(stream_key, shape, split, -0.22, 0.18) * entries
    return jnp.clip(entries, min=-bound, max=bound).astype(held_as)


def setup_inputs(seed: int = 0, part: int = 0) -> dict:
    streams_of = jax.random.split(jax.random.key(seed), 5)
    own_keys = jax.random.split(jax.random.fold_in(streams_of[4], part), 5)
    return {
        "latents": normal_values(own_keys[0], (FRAMES, HEIGHT, C, W), 1.0, 6.0, ((0, 4), (1, 4))),
        "conv_weight": normal_values(streams_of[1], (LAYERS, 27, C, C), (27 * C) ** -0.5, 0.078125),
        "norm_gains": jnp.clip(jax.random.uniform(streams_of[2], (LAYERS, C), jnp.float32, 0.5, 1.5), 0.5, 1.5),
        "biases": normal_values(streams_of[3], (LAYERS, C), 0.5, 3.0, (), jnp.float32),
    }


EPSILON = 1e-06

def activate(values, gain_row):
    widened = values.astype(jnp.float32)
    squares = lax.optimization_barrier(jnp.mean(widened * widened, axis=2, keepdims=True))
    normed = widened * lax.rsqrt(squares + EPSILON) * gain_row[None, None, :, None]
    return jax.nn.silu(normed).astype(jnp.bfloat16)

def one_layer(values, gain_row, weight, bias_row):
    rounded = activate(values, gain_row)
    padded = jnp.pad(lax.optimization_barrier(rounded).astype(jnp.float32), ((2, 0), (1, 1), (0, 0), (1, 1)))
    frames = values.shape[0]
    height = values.shape[1]
    columns = values.shape[3]
    total = jnp.zeros(values.shape, jnp.float32)
    for time_tap in range(3):
        for row_tap in range(3):
            for column_tap in range(3):
                window = padded[time_tap:time_tap + frames, row_tap:row_tap + height, :, column_tap:column_tap + columns]
                kernel = weight[9 * time_tap + 3 * row_tap + column_tap].astype(jnp.float32)
                total = total + jnp.einsum('oc,fhcw->fhow', kernel, window, precision=lax.Precision.HIGHEST)
    summed = values.astype(jnp.float32) + total + bias_row[None, None, :, None]
    return summed.astype(jnp.bfloat16)

def reference(latents, conv_weight, norm_gains, biases):
    values = latents
    for layer_index in range(LAYERS):
        values = one_layer(values, norm_gains[layer_index], conv_weight[layer_index], biases[layer_index])
    return values
```

```python
import functools

import jax
import jax.numpy as jnp
from jax import lax
from jax.experimental import pallas as pl
from jax.experimental.pallas import tpu as pltpu
from jax.sharding import PartitionSpec as P

EPSILON = 1e-06
MESH = pl.DeviceIdType.MESH

TM, UP = 0, 2


def stack_kernel(
    layers, frames, rows_here, channels, columns,
    x_ref, w_hbm, gains_ref, biases_ref, out_ref,
    w_raw, w_cat, act, values, gain_col, bias_col,
    w_sem, send_sem, recv_sem,
):
    tm, tm_count = lax.axis_index("tm"), lax.axis_size("tm")
    row, row_count = lax.axis_index("rows"), lax.axis_size("rows")
    has_prev, has_next = tm > 0, tm < tm_count - 1
    has_up, has_down = row > 0, row < row_count - 1
    last_row = rows_here
    DOWN = UP + frames + 2

    def weights(layer):
        return pltpu.make_async_copy(w_hbm.at[layer], w_raw.at[layer], w_sem.at[layer])

    for layer in range(layers):
        weights(layer).start()

    barrier = pltpu.get_barrier_semaphore()
    for there, target in (
        (has_prev, {"tm": tm - 1}),
        (has_next, {"tm": tm + 1}),
        (has_up, {"rows": row - 1}),
        (has_down, {"rows": row + 1}),
    ):
        @pl.when(there)
        def _(target=target):
            pl.semaphore_signal(barrier, inc=1, device_id=target, device_id_type=MESH)

    def tm_copy(layer, frame):
        at = frame - (frames - 2)
        return pltpu.make_async_remote_copy(
            src_ref=act.at[layer, frame + 2, pl.ds(1, rows_here)],
            dst_ref=act.at[layer, at, pl.ds(1, rows_here)],
            send_sem=send_sem.at[layer, TM + at],
            recv_sem=recv_sem.at[layer, TM + at],
            device_id={"tm": tm + 1},
            device_id_type=MESH,
        )

    def up_copy(layer, padded):
        return pltpu.make_async_remote_copy(
            src_ref=act.at[layer, padded, 1],
            dst_ref=act.at[layer, padded, last_row + 1],
            send_sem=send_sem.at[layer, UP + padded],
            recv_sem=recv_sem.at[layer, UP + padded],
            device_id={"rows": row - 1},
            device_id_type=MESH,
        )

    def down_copy(layer, padded):
        return pltpu.make_async_remote_copy(
            src_ref=act.at[layer, padded, last_row],
            dst_ref=act.at[layer, padded, 0],
            send_sem=send_sem.at[layer, DOWN + padded],
            recv_sem=recv_sem.at[layer, DOWN + padded],
            device_id={"rows": row + 1},
            device_id_type=MESH,
        )

    def send_rows(layer, padded):
        @pl.when(has_up)
        def _():
            up_copy(layer, padded).start()

        @pl.when(has_down)
        def _():
            down_copy(layer, padded).start()

    def wait_rows(layer, padded):
        @pl.when(has_down)
        def _():
            up_copy(layer, padded).wait_recv()

        @pl.when(has_up)
        def _():
            down_copy(layer, padded).wait_recv()

    def activate(layer, frame, value):
        squares = jnp.mean(value * value, axis=1, keepdims=True)
        normed = value * lax.rsqrt(squares + EPSILON) * gain_col[layer][None]
        act[layer, frame + 2, pl.ds(1, rows_here)] = (
            normed / (1.0 + jnp.exp(-normed))
        ).astype(jnp.bfloat16)

    def send_frame(layer, frame):
        if frame >= frames - 2:
            @pl.when(has_next)
            def _():
                tm_copy(layer, frame).start()
        send_rows(layer, frame + 2)

    def relay(layer, at):
        @pl.when(has_prev)
        def _():
            tm_copy(layer, at + frames - 2).wait_recv()
            send_rows(layer, at)

    def prepare(layer):
        weights(layer).wait()
        taps = w_raw.shape[1] // 3
        for c in range(3):
            for first in range(0, taps, 2):
                count = min(2, taps - first)
                tiles = [w_raw[layer, 3 * (first + n) + c] for n in range(count)]
                block = jnp.concatenate(tiles, axis=1) if count > 1 else tiles[0]
                w_cat[
                    layer,
                    c * channels:(c + 1) * channels,
                    first * channels:(first + count) * channels,
                ] = block

    def columns_of(ref, layer):
        line = ref[pl.ds(layer, 1), :]
        return jnp.transpose(jnp.broadcast_to(line, (columns, channels)))

    for layer in range(layers):
        gain_col[layer] = columns_of(gains_ref, layer)
        bias_col[layer] = columns_of(biases_ref, layer)

    for frame in range(frames - 1, -1, -1):
        activate(0, frame, x_ref[frame].astype(jnp.float32))

    greeted = sum(there.astype(jnp.int32) for there in (has_prev, has_next, has_up, has_down))
    pl.semaphore_wait(barrier, greeted)
    for frame in range(frames - 1, -1, -1):
        send_frame(0, frame)

    zero_frame = jnp.zeros((channels, columns), jnp.bfloat16)
    for layer in range(layers):
        @pl.when(jnp.logical_not(has_prev))
        def _(layer=layer):
            for at in range(2):
                for h in range(rows_here + 2):
                    act[layer, at, h] = zero_frame

        @pl.when(jnp.logical_and(has_prev, jnp.logical_not(has_up)))
        def _(layer=layer):
            for at in range(2):
                act[layer, at, 0] = zero_frame

        @pl.when(jnp.logical_and(has_prev, jnp.logical_not(has_down)))
        def _(layer=layer):
            for at in range(2):
                act[layer, at, last_row + 1] = zero_frame

        @pl.when(jnp.logical_not(has_up))
        def _(layer=layer):
            for at in range(frames):
                act[layer, at + 2, 0] = zero_frame

        @pl.when(jnp.logical_not(has_down))
        def _(layer=layer):
            for at in range(frames):
                act[layer, at + 2, last_row + 1] = zero_frame

    prepare(0)

    lane = lax.broadcasted_iota(jnp.int32, (channels, columns), 1)
    not_first, not_last = lane > 0, lane < columns - 1
    depth = 9 * channels

    def convolve(layer, frame):
        rhs = jnp.concatenate(
            [
                act[layer, frame:frame + 3, h:h + 3].reshape(depth, columns)
                for h in range(rows_here)
            ],
            axis=1,
        )
        product = jnp.dot(w_cat[layer], rhs, preferred_element_type=jnp.float32)
        results = []
        for h in range(rows_here):
            part = product[:, h * columns:(h + 1) * columns]
            left = pltpu.roll(part[:channels], 1, 1)
            right = pltpu.roll(part[2 * channels:], columns - 1, 1)
            total = part[channels:2 * channels]
            total = total + jnp.where(not_first, left, 0.0)
            total = total + jnp.where(not_last, right, 0.0)
            before = x_ref[frame, h] if layer == 0 else values[frame, h]
            summed = before.astype(jnp.float32) + total + bias_col[layer]
            results.append(summed.astype(jnp.bfloat16))
        return results

    for layer in range(layers):
        for frame in range(frames - 1, -1, -1):
            if frame == 2:
                relay(layer, 1)
            if frame == 1:
                relay(layer, 0)
                if layer == 0:
                    for later in range(1, layers):
                        prepare(later)
            if frame == frames - 1:
                for padded in range(frames + 1, frame - 1, -1):
                    wait_rows(layer, padded)
            elif frame >= 2:
                wait_rows(layer, frame)
            else:
                @pl.when(has_prev)
                def _(layer=layer, frame=frame):
                    wait_rows(layer, frame)
            results = convolve(layer, frame)
            if layer == layers - 1:
                for h in range(rows_here):
                    out_ref[frame, h] = results[h]
            else:
                for h in range(rows_here):
                    values[frame, h] = results[h]
                activate(layer + 1, frame, jnp.stack(results).astype(jnp.float32))
                send_frame(layer + 1, frame)

    for layer in range(layers):
        for frame in (frames - 1, frames - 2):
            @pl.when(has_next)
            def _(layer=layer, frame=frame):
                tm_copy(layer, frame).wait_send()
        for padded in range(frames + 2):
            there = True if padded >= 2 else has_prev

            @pl.when(jnp.logical_and(has_up, there))
            def _(layer=layer, padded=padded):
                up_copy(layer, padded).wait_send()

            @pl.when(jnp.logical_and(has_down, there))
            def _(layer=layer, padded=padded):
                down_copy(layer, padded).wait_send()


def on_device(latents, conv_weight, norm_gains, biases):
    frames, rows_here, channels, columns = latents.shape
    layers, taps = conv_weight.shape[:2]
    kinds = 2 + 2 * (frames + 2)
    vmem = pl.BlockSpec(memory_space=pltpu.VMEM)
    return pl.pallas_call(
        functools.partial(stack_kernel, layers, frames, rows_here, channels, columns),
        out_shape=jax.ShapeDtypeStruct(latents.shape, latents.dtype),
        in_specs=[vmem, pl.BlockSpec(memory_space=pl.ANY), vmem, vmem],
        out_specs=vmem,
        scratch_shapes=[
            pltpu.VMEM((layers, taps, channels, channels), jnp.bfloat16),
            pltpu.VMEM((layers, 3 * channels, 9 * channels), jnp.bfloat16),
            pltpu.VMEM((layers, frames + 2, rows_here + 2, channels, columns), jnp.bfloat16),
            pltpu.VMEM((frames, rows_here, channels, columns), jnp.bfloat16),
            pltpu.VMEM((layers, channels, columns), jnp.float32),
            pltpu.VMEM((layers, channels, columns), jnp.float32),
            pltpu.SemaphoreType.DMA((layers,)),
            pltpu.SemaphoreType.DMA((layers, kinds)),
            pltpu.SemaphoreType.DMA((layers, kinds)),
        ],
        compiler_params=pltpu.CompilerParams(collective_id=0, has_side_effects=True),
        name="conv_stack",
    )(latents, conv_weight, norm_gains, biases)


def solution(mesh):
    in_specs = (P(("clips", "tm"), "rows", None, None), P(), P(), P())
    out_specs = P(("clips", "tm"), "rows", None, None)
    return jax.shard_map(
        on_device, mesh=mesh, in_specs=in_specs, out_specs=out_specs, check_vma=False
    )
```

```python
import functools

import jax
import jax.numpy as jnp
from jax import lax
from jax.experimental import pallas as pl
from jax.experimental.pallas import tpu as pltpu
from jax.sharding import PartitionSpec as P

EPSILON = 1e-06
MESH = pl.DeviceIdType.MESH

TM, UP = 0, 2


def stack_kernel(
    layers, frames, rows_here, channels, columns,
    x_ref, w_hbm, gains_ref, biases_ref, out_ref,
    w_raw, w_cat, early, products, act, values, gain_col, bias_col,
    w_sem, send_sem, recv_sem,
):
    tm, tm_count = lax.axis_index("tm"), lax.axis_size("tm")
    row, row_count = lax.axis_index("rows"), lax.axis_size("rows")
    has_prev, has_next = tm > 0, tm < tm_count - 1
    has_up, has_down = row > 0, row < row_count - 1
    last_row = rows_here
    DOWN = UP + frames + 2

    def weights(layer):
        return pltpu.make_async_copy(w_hbm.at[layer], w_raw.at[layer], w_sem.at[layer])

    for layer in range(layers):
        weights(layer).start()

    barrier = pltpu.get_barrier_semaphore()
    for there, target in (
        (has_prev, {"tm": tm - 1}),
        (has_next, {"tm": tm + 1}),
        (has_up, {"rows": row - 1}),
        (has_down, {"rows": row + 1}),
    ):
        @pl.when(there)
        def _(target=target):
            pl.semaphore_signal(barrier, inc=1, device_id=target, device_id_type=MESH)

    def tm_copy(layer, frame):
        at = frame - (frames - 2)
        return pltpu.make_async_remote_copy(
            src_ref=act.at[layer, frame + 2, pl.ds(1, rows_here)],
            dst_ref=act.at[layer, at, pl.ds(1, rows_here)],
            send_sem=send_sem.at[layer, TM + at],
            recv_sem=recv_sem.at[layer, TM + at],
            device_id={"tm": tm + 1},
            device_id_type=MESH,
        )

    def up_copy(layer, padded):
        return pltpu.make_async_remote_copy(
            src_ref=act.at[layer, padded, 1],
            dst_ref=act.at[layer, padded, last_row + 1],
            send_sem=send_sem.at[layer, UP + padded],
            recv_sem=recv_sem.at[layer, UP + padded],
            device_id={"rows": row - 1},
            device_id_type=MESH,
        )

    def down_copy(layer, padded):
        return pltpu.make_async_remote_copy(
            src_ref=act.at[layer, padded, last_row],
            dst_ref=act.at[layer, padded, 0],
            send_sem=send_sem.at[layer, DOWN + padded],
            recv_sem=recv_sem.at[layer, DOWN + padded],
            device_id={"rows": row + 1},
            device_id_type=MESH,
        )

    def send_rows(layer, padded):
        @pl.when(has_up)
        def _():
            up_copy(layer, padded).start()

        @pl.when(has_down)
        def _():
            down_copy(layer, padded).start()

    def wait_rows(layer, padded):
        @pl.when(has_down)
        def _():
            up_copy(layer, padded).wait_recv()

        @pl.when(has_up)
        def _():
            down_copy(layer, padded).wait_recv()

    def activate(layer, frame, value):
        squares = jnp.mean(value * value, axis=1, keepdims=True)
        half = value * lax.rsqrt(squares + EPSILON) * gain_col[layer][None]
        act[layer, frame + 2, pl.ds(1, rows_here)] = (
            half + half * jnp.tanh(half)
        ).astype(jnp.bfloat16)

    def send_frame(layer, frame):
        if frame >= frames - 2:
            @pl.when(has_next)
            def _():
                tm_copy(layer, frame).start()
        send_rows(layer, frame + 2)

    def relay(layer, at):
        @pl.when(has_prev)
        def _():
            tm_copy(layer, at + frames - 2).wait_recv()
            send_rows(layer, at)

    def prepare(layer):
        weights(layer).wait()
        taps = w_raw.shape[1] // 3
        order = [3 * a + b for a in (2, 1, 0) for b in range(3)]
        for c in range(3):
            for first in range(0, taps, 2):
                count = min(2, taps - first)
                tiles = [w_raw[layer, 3 * order[first + n] + c] for n in range(count)]
                block = jnp.concatenate(tiles, axis=1) if count > 1 else tiles[0]
                w_cat[
                    layer,
                    c * channels:(c + 1) * channels,
                    first * channels:(first + count) * channels,
                ] = block

    def columns_of(ref, layer):
        line = ref[pl.ds(layer, 1), :]
        return jnp.transpose(jnp.broadcast_to(line, (columns, channels)))

    gain_col[0] = 0.5 * columns_of(gains_ref, 0)
    activate(0, frames - 1, x_ref[frames - 1].astype(jnp.float32))
    greeted = sum(there.astype(jnp.int32) for there in (has_prev, has_next, has_up, has_down))
    pl.semaphore_wait(barrier, greeted)
    send_frame(0, frames - 1)
    for frame in range(frames - 2, -1, -1):
        activate(0, frame, x_ref[frame].astype(jnp.float32))
        send_frame(0, frame)
    for layer in range(layers):
        if layer > 0:
            gain_col[layer] = 0.5 * columns_of(gains_ref, layer)
        bias_col[layer] = columns_of(biases_ref, layer)

    zero_frame = jnp.zeros((channels, columns), jnp.bfloat16)
    for layer in range(layers):
        @pl.when(jnp.logical_not(has_prev))
        def _(layer=layer):
            for at in range(2):
                for h in range(rows_here + 2):
                    act[layer, at, h] = zero_frame

        @pl.when(jnp.logical_and(has_prev, jnp.logical_not(has_up)))
        def _(layer=layer):
            for at in range(2):
                act[layer, at, 0] = zero_frame

        @pl.when(jnp.logical_and(has_prev, jnp.logical_not(has_down)))
        def _(layer=layer):
            for at in range(2):
                act[layer, at, last_row + 1] = zero_frame

        @pl.when(jnp.logical_not(has_up))
        def _(layer=layer):
            for at in range(frames):
                act[layer, at + 2, 0] = zero_frame

        @pl.when(jnp.logical_not(has_down))
        def _(layer=layer):
            for at in range(frames):
                act[layer, at + 2, last_row + 1] = zero_frame

    prepare(0)

    lane = lax.broadcasted_iota(jnp.int32, (channels, columns), 1)
    not_first, not_last = lane > 0, lane < columns - 1
    local_depth = 6 * channels

    def windows(layer, frame, taps):
        return jnp.concatenate(
            [
                jnp.concatenate(
                    [
                        act[layer, frame + a, h:h + 3].reshape(3 * channels, columns)
                        for a in taps
                    ],
                    axis=0,
                )
                for h in range(rows_here)
            ],
            axis=1,
        )

    def local_part(layer, frame):
        early[...] = jnp.dot(
            w_cat[layer, :, :local_depth],
            windows(layer, frame, (2, 1)),
            preferred_element_type=jnp.float32,
        )

    def multiply(layer, frame, resumed):
        if resumed:
            return early[...] + jnp.dot(
                w_cat[layer, :, local_depth:],
                windows(layer, frame, (0,)),
                preferred_element_type=jnp.float32,
            )
        return jnp.dot(
            w_cat[layer], windows(layer, frame, (2, 1, 0)), preferred_element_type=jnp.float32
        )

    def finish(layer, frame, product):
        results = []
        for h in range(rows_here):
            part = product[:, h * columns:(h + 1) * columns]
            left = pltpu.roll(part[:channels], 1, 1)
            right = pltpu.roll(part[2 * channels:], columns - 1, 1)
            total = part[channels:2 * channels]
            total = total + jnp.where(not_first, left, 0.0)
            total = total + jnp.where(not_last, right, 0.0)
            before = x_ref[frame, h] if layer == 0 else values[frame, h]
            summed = before.astype(jnp.float32) + total + bias_col[layer]
            results.append(summed.astype(jnp.bfloat16))
        into = out_ref if layer == layers - 1 else values
        for h in range(rows_here):
            into[frame, h] = results[h]
        if layer < layers - 1:
            activate(layer + 1, frame, jnp.stack(results).astype(jnp.float32))

    def send_next(layer, frame):
        if layer < layers - 1:
            send_frame(layer + 1, frame)

    for layer in range(layers):
        pending = None
        for frame in range(frames - 1, -1, -1):
            resumed = layer == 0 and frame == 1
            late = frame <= 1
            if frame == (1 if layer == 0 else 2):
                relay(layer, 1)
            if resumed:
                for later in range(1, layers):
                    prepare(later)
                local_part(layer, frame)
                if pending is not None:
                    finish(layer, pending, products[pending % 2])
                    send_next(layer, pending)
                    pending = None
            if frame == 1:
                relay(layer, 0)
            if frame == frames - 1:
                for padded in range(frames + 1, frame - 1, -1):
                    wait_rows(layer, padded)
            elif frame >= 2:
                wait_rows(layer, frame)
            else:
                @pl.when(has_prev)
                def _(layer=layer, frame=frame):
                    wait_rows(layer, frame)
            product = multiply(layer, frame, resumed)
            if pending is not None:
                finish(layer, pending, products[pending % 2])
            hold = frame > 0 if layer == layers - 1 else not late
            if hold:
                products[frame % 2] = product
            else:
                finish(layer, frame, product)
            if pending is not None:
                send_next(layer, pending)
                pending = None
            if hold:
                pending = frame
            else:
                send_next(layer, frame)

    for layer in range(layers):
        for frame in (frames - 1, frames - 2):
            @pl.when(has_next)
            def _(layer=layer, frame=frame):
                tm_copy(layer, frame).wait_send()
        for padded in range(frames + 2):
            there = True if padded >= 2 else has_prev

            @pl.when(jnp.logical_and(has_up, there))
            def _(layer=layer, padded=padded):
                up_copy(layer, padded).wait_send()

            @pl.when(jnp.logical_and(has_down, there))
            def _(layer=layer, padded=padded):
                down_copy(layer, padded).wait_send()


def on_device(latents, conv_weight, norm_gains, biases):
    frames, rows_here, channels, columns = latents.shape
    layers, taps = conv_weight.shape[:2]
    kinds = 2 + 2 * (frames + 2)
    vmem = pl.BlockSpec(memory_space=pltpu.VMEM)
    return pl.pallas_call(
        functools.partial(stack_kernel, layers, frames, rows_here, channels, columns),
        out_shape=jax.ShapeDtypeStruct(latents.shape, latents.dtype),
        in_specs=[vmem, pl.BlockSpec(memory_space=pl.ANY), vmem, vmem],
        out_specs=vmem,
        scratch_shapes=[
            pltpu.VMEM((layers, taps, channels, channels), jnp.bfloat16),
            pltpu.VMEM((layers, 3 * channels, 9 * channels), jnp.bfloat16),
            pltpu.VMEM((3 * channels, rows_here * columns), jnp.float32),
            pltpu.VMEM((2, 3 * channels, rows_here * columns), jnp.float32),
            pltpu.VMEM((layers, frames + 2, rows_here + 2, channels, columns), jnp.bfloat16),
            pltpu.VMEM((frames, rows_here, channels, columns), jnp.bfloat16),
            pltpu.VMEM((layers, channels, columns), jnp.float32),
            pltpu.VMEM((layers, channels, columns), jnp.float32),
            pltpu.SemaphoreType.DMA((layers,)),
            pltpu.SemaphoreType.DMA((layers, kinds)),
            pltpu.SemaphoreType.DMA((layers, kinds)),
        ],
        compiler_params=pltpu.CompilerParams(collective_id=0, has_side_effects=True),
        name="conv_stack",
    )(latents, conv_weight, norm_gains, biases)


def solution(mesh):
    in_specs = (P(("clips", "tm"), "rows", None, None), P(), P(), P())
    out_specs = P(("clips", "tm"), "rows", None, None)
    return jax.shard_map(
        on_device, mesh=mesh, in_specs=in_specs, out_specs=out_specs, check_vma=False
    )
```

```python
import functools

import jax
import jax.numpy as jnp
from jax import lax
from jax.experimental import pallas as pl
from jax.experimental.pallas import tpu as pltpu
from jax.sharding import PartitionSpec as P

EPSILON = 1e-06
MESH = pl.DeviceIdType.MESH

TM, UP = 0, 2


def stack_kernel(
    layers, frames, rows_here, channels, columns,
    x_ref, w_hbm, gains_ref, biases_ref, out_ref,
    w_raw, w_cat, early, products, act, values, gain_col, bias_col,
    w_sem, send_sem, recv_sem,
):
    tm, tm_count = lax.axis_index("tm"), lax.axis_size("tm")
    row, row_count = lax.axis_index("rows"), lax.axis_size("rows")
    has_prev, has_next = tm > 0, tm < tm_count - 1
    has_up, has_down = row > 0, row < row_count - 1
    last_row = rows_here
    DOWN = UP + frames + 2

    def weights(layer):
        return pltpu.make_async_copy(w_hbm.at[layer], w_raw.at[layer], w_sem.at[layer])

    for layer in range(layers):
        weights(layer).start()

    barrier = pltpu.get_barrier_semaphore()
    for there, target in (
        (has_prev, {"tm": tm - 1}),
        (has_next, {"tm": tm + 1}),
        (has_up, {"rows": row - 1}),
        (has_down, {"rows": row + 1}),
    ):
        @pl.when(there)
        def _(target=target):
            pl.semaphore_signal(barrier, inc=1, device_id=target, device_id_type=MESH)

    def tm_copy(layer, frame):
        at = frame - (frames - 2)
        return pltpu.make_async_remote_copy(
            src_ref=act.at[layer, frame + 2, pl.ds(1, rows_here)],
            dst_ref=act.at[layer, at, pl.ds(1, rows_here)],
            send_sem=send_sem.at[layer, TM + at],
            recv_sem=recv_sem.at[layer, TM + at],
            device_id={"tm": tm + 1},
            device_id_type=MESH,
        )

    def up_copy(layer, padded):
        return pltpu.make_async_remote_copy(
            src_ref=act.at[layer, padded, 1],
            dst_ref=act.at[layer, padded, last_row + 1],
            send_sem=send_sem.at[layer, UP + padded],
            recv_sem=recv_sem.at[layer, UP + padded],
            device_id={"rows": row - 1},
            device_id_type=MESH,
        )

    def down_copy(layer, padded):
        return pltpu.make_async_remote_copy(
            src_ref=act.at[layer, padded, last_row],
            dst_ref=act.at[layer, padded, 0],
            send_sem=send_sem.at[layer, DOWN + padded],
            recv_sem=recv_sem.at[layer, DOWN + padded],
            device_id={"rows": row + 1},
            device_id_type=MESH,
        )

    def send_rows(layer, padded):
        @pl.when(has_up)
        def _():
            up_copy(layer, padded).start()

        @pl.when(has_down)
        def _():
            down_copy(layer, padded).start()

    def wait_rows(layer, padded):
        @pl.when(has_down)
        def _():
            up_copy(layer, padded).wait_recv()

        @pl.when(has_up)
        def _():
            down_copy(layer, padded).wait_recv()

    def activate(layer, frame, value):
        squares = jnp.mean(value * value, axis=1, keepdims=True)
        half = value * lax.rsqrt(squares + EPSILON) * gain_col[layer][None]
        act[layer, frame + 2, pl.ds(1, rows_here)] = (
            half + half * jnp.tanh(half)
        ).astype(jnp.bfloat16)

    def send_frame(layer, frame):
        if frame >= frames - 2:
            @pl.when(has_next)
            def _():
                tm_copy(layer, frame).start()
        send_rows(layer, frame + 2)

    def relay(layer, at):
        @pl.when(has_prev)
        def _():
            tm_copy(layer, at + frames - 2).wait_recv()
            send_rows(layer, at)

    def prepare(layer):
        weights(layer).wait()
        taps = w_raw.shape[1] // 3
        order = [3 * a + b for a in (2, 1, 0) for b in range(3)]
        for c in range(3):
            for first in range(0, taps, 2):
                count = min(2, taps - first)
                tiles = [w_raw[layer, 3 * order[first + n] + c] for n in range(count)]
                block = jnp.concatenate(tiles, axis=1) if count > 1 else tiles[0]
                w_cat[
                    layer,
                    c * channels:(c + 1) * channels,
                    first * channels:(first + count) * channels,
                ] = block

    def columns_of(ref, layer):
        line = ref[pl.ds(layer, 1), :]
        return jnp.transpose(jnp.broadcast_to(line, (columns, channels)))

    gain_col[0] = 0.5 * columns_of(gains_ref, 0)
    activate(0, frames - 1, x_ref[frames - 1].astype(jnp.float32))
    greeted = sum(there.astype(jnp.int32) for there in (has_prev, has_next, has_up, has_down))
    pl.semaphore_wait(barrier, greeted)
    send_frame(0, frames - 1)
    for frame in range(frames - 2, -1, -1):
        activate(0, frame, x_ref[frame].astype(jnp.float32))
        send_frame(0, frame)
    for layer in range(layers):
        if layer > 0:
            gain_col[layer] = 0.5 * columns_of(gains_ref, layer)
        bias_col[layer] = columns_of(biases_ref, layer)

    zero_frame = jnp.zeros((channels, columns), jnp.bfloat16)
    for layer in range(layers):
        @pl.when(jnp.logical_not(has_prev))
        def _(layer=layer):
            for at in range(2):
                for h in range(rows_here + 2):
                    act[layer, at, h] = zero_frame

        @pl.when(jnp.logical_and(has_prev, jnp.logical_not(has_up)))
        def _(layer=layer):
            for at in range(2):
                act[layer, at, 0] = zero_frame

        @pl.when(jnp.logical_and(has_prev, jnp.logical_not(has_down)))
        def _(layer=layer):
            for at in range(2):
                act[layer, at, last_row + 1] = zero_frame

        @pl.when(jnp.logical_not(has_up))
        def _(layer=layer):
            for at in range(frames):
                act[layer, at + 2, 0] = zero_frame

        @pl.when(jnp.logical_not(has_down))
        def _(layer=layer):
            for at in range(frames):
                act[layer, at + 2, last_row + 1] = zero_frame

    prepare(0)

    lane = lax.broadcasted_iota(jnp.int32, (channels, columns), 1)
    not_first, not_last = lane > 0, lane < columns - 1
    local_depth = 6 * channels

    def windows(layer, frame, taps):
        return jnp.concatenate(
            [
                jnp.concatenate(
                    [
                        act[layer, frame + a, h:h + 3].reshape(3 * channels, columns)
                        for a in taps
                    ],
                    axis=0,
                )
                for h in range(rows_here)
            ],
            axis=1,
        )

    def local_part(layer, frame):
        early[...] = jnp.dot(
            w_cat[layer, :, :local_depth],
            windows(layer, frame, (2, 1)),
            preferred_element_type=jnp.float32,
        )

    def multiply(layer, frame, resumed):
        if resumed:
            return early[...] + jnp.dot(
                w_cat[layer, :, local_depth:],
                windows(layer, frame, (0,)),
                preferred_element_type=jnp.float32,
            )
        return jnp.dot(
            w_cat[layer], windows(layer, frame, (2, 1, 0)), preferred_element_type=jnp.float32
        )

    def finish(layer, frame, product):
        results = []
        for h in range(rows_here):
            part = product[:, h * columns:(h + 1) * columns]
            left = pltpu.roll(part[:channels], 1, 1)
            right = pltpu.roll(part[2 * channels:], columns - 1, 1)
            total = part[channels:2 * channels]
            total = total + jnp.where(not_first, left, 0.0)
            total = total + jnp.where(not_last, right, 0.0)
            before = x_ref[frame, h] if layer == 0 else values[frame, h]
            summed = before.astype(jnp.float32) + total + bias_col[layer]
            results.append(summed.astype(jnp.bfloat16))
        into = out_ref if layer == layers - 1 else values
        for h in range(rows_here):
            into[frame, h] = results[h]
        if layer < layers - 1:
            activate(layer + 1, frame, jnp.stack(results).astype(jnp.float32))

    def send_next(layer, frame):
        if layer < layers - 1:
            send_frame(layer + 1, frame)

    for layer in range(layers):
        pending = None
        for frame in range(frames - 1, -1, -1):
            resumed = layer == 0 and frame == 1
            if layer == 0 and frame == 1:
                relay(layer, 1)
            if resumed:
                for later in range(1, layers):
                    prepare(later)
                local_part(layer, frame)
                if pending is not None:
                    finish(layer, pending, products[pending % 2])
                    send_next(layer, pending)
                    pending = None
            if layer == 0 and frame == 1:
                relay(layer, 0)
            if frame == frames - 1:
                for padded in range(frames + 1, frame - 1, -1):
                    wait_rows(layer, padded)
            elif frame >= 2:
                wait_rows(layer, frame)
            else:
                @pl.when(has_prev)
                def _(layer=layer, frame=frame):
                    wait_rows(layer, frame)
            if layer > 0 and frame >= frames - 2:
                relay(layer, frame - (frames - 2))
            product = multiply(layer, frame, resumed)
            if pending is not None:
                finish(layer, pending, products[pending % 2])
            hold = layer == layers - 1 and frame > 0
            if hold:
                products[frame % 2] = product
            else:
                finish(layer, frame, product)
            if pending is not None:
                send_next(layer, pending)
                pending = None
            if hold:
                pending = frame
            else:
                send_next(layer, frame)

    for layer in range(layers):
        for frame in (frames - 1, frames - 2):
            @pl.when(has_next)
            def _(layer=layer, frame=frame):
                tm_copy(layer, frame).wait_send()
        for padded in range(frames + 2):
            there = True if padded >= 2 else has_prev

            @pl.when(jnp.logical_and(has_up, there))
            def _(layer=layer, padded=padded):
                up_copy(layer, padded).wait_send()

            @pl.when(jnp.logical_and(has_down, there))
            def _(layer=layer, padded=padded):
                down_copy(layer, padded).wait_send()


def on_device(latents, conv_weight, norm_gains, biases):
    frames, rows_here, channels, columns = latents.shape
    layers, taps = conv_weight.shape[:2]
    kinds = 2 + 2 * (frames + 2)
    vmem = pl.BlockSpec(memory_space=pltpu.VMEM)
    return pl.pallas_call(
        functools.partial(stack_kernel, layers, frames, rows_here, channels, columns),
        out_shape=jax.ShapeDtypeStruct(latents.shape, latents.dtype),
        in_specs=[vmem, pl.BlockSpec(memory_space=pl.ANY), vmem, vmem],
        out_specs=vmem,
        scratch_shapes=[
            pltpu.VMEM((layers, taps, channels, channels), jnp.bfloat16),
            pltpu.VMEM((layers, 3 * channels, 9 * channels), jnp.bfloat16),
            pltpu.VMEM((3 * channels, rows_here * columns), jnp.float32),
            pltpu.VMEM((2, 3 * channels, rows_here * columns), jnp.float32),
            pltpu.VMEM((layers, frames + 2, rows_here + 2, channels, columns), jnp.bfloat16),
            pltpu.VMEM((frames, rows_here, channels, columns), jnp.bfloat16),
            pltpu.VMEM((layers, channels, columns), jnp.float32),
            pltpu.VMEM((layers, channels, columns), jnp.float32),
            pltpu.SemaphoreType.DMA((layers,)),
            pltpu.SemaphoreType.DMA((layers, kinds)),
            pltpu.SemaphoreType.DMA((layers, kinds)),
        ],
        compiler_params=pltpu.CompilerParams(collective_id=0, has_side_effects=True),
        name="conv_stack",
    )(latents, conv_weight, norm_gains, biases)


def solution(mesh):
    in_specs = (P(("clips", "tm"), "rows", None, None), P(), P(), P())
    out_specs = P(("clips", "tm"), "rows", None, None)
    return jax.shard_map(
        on_device, mesh=mesh, in_specs=in_specs, out_specs=out_specs, check_vma=False
    )
```
